32 devices in a mesh: wa: 8 (over y, x, core), gz: 4 (over z).
Axes of the slice: x: 2, y: 2, z: 4, core: 2. Of those that a mesh axis runs over, the one named last changes fastest.
Arguments:
- velocity_modes: float32 [2, 8, 512, 512], P(None, 'gz', 'wa'), may hold values from -0.03125 to 0.03125
- scalar: float32 [16, 1024, 1024], P('gz', 'wa'), may hold values from -3 to 3
- nest_shift: int32 [1], replicated, may hold values from 0 to 1023
Outputs:
- stress: bfloat16 [2, 8, 512, 512], P(None, 'gz', 'wa')
- scalar_next: float32 [16, 1024, 1024], P('gz', 'wa')
The draws below stay inside these ranges and needn't reach their ends.
Inputs may be any that keep to these rules, and one draw needn't show every extreme that they name: `nest_shift`: a shift of the fine grid along x in fine cells.
All inputs are finite; a program needn't handle non-finite values.
Results may differ from the reference program's by a relative error of at most 0.001.
Values sent between devices are 32-bit elements; how exact they have to be, the bound alone decides.
A program may use at most 128 MiB of HBM per device.

```python
import math
import jax
import jax.numpy as jnp
from jax import lax

KX = 512
KY = 512
NPX = 768
NPY = 768
FX = 1024
FY = 1024
CZ = 8
FZ = 16


def steps_of(rng, shape, split, low, largest):
    gain = 1.0
    for position, shards_of in split:
        draws = jax.random.uniform(jax.random.fold_in(jax.random.fold_in(rng, 6), position), (shards_of,), jnp.float32, low / len(split), largest / len(split))
        gain = gain * jnp.repeat(jnp.exp(draws), shape[position] // shards_of).reshape((-1,) + (1,) * (len(shape) - 1 - position))
    return gain


def normal_values(own_key, shape, deviation, bound, pieces=(), kind=jnp.bfloat16):
    array = jax.random.normal(own_key, shape, jnp.float32) * deviation
    if len(pieces) > 0:
        array = steps_of(own_key, shape, pieces, -0.22, 0.18) * array
    return jnp.clip(array, min=-bound, max=bound).astype(kind)


def setup_inputs(seed: int = 0) -> dict:
    key_list = jax.random.split(jax.random.key(seed), 4)
    return {
        "velocity_modes": normal_values(key_list[0], (2, CZ, KX, KY), ((KX * KY) ** -0.5), 0.03125, ((1, 4), (2, 8)), jnp.float32),
        "scalar": normal_values(key_list[1], (FZ, FY, FX), 1.0, 3.0, ((0, 4), (1, 8)), jnp.float32),
        "nest_shift": jax.random.randint(key_list[2], (1,), 0, FX).astype(jnp.int32),
    }


kappa_base = 0.1
time_step = 0.2
highest = lax.Precision.HIGHEST

def signed_mode(number, length):
    return jnp.where(number < length // 2, number, number - length)

def hartley_table(modes_in, points, length):
    phase = jnp.mod(modes_in * points, length).astype(jnp.float32) * (2.0 * math.pi / length)
    return jnp.cos(phase) + jnp.sin(phase)

def cubic_weights(fraction):
    square = fraction * fraction
    cube = square * fraction
    return ((-cube + 2.0 * square - fraction) * 0.5, (3.0 * cube - 5.0 * square + 2.0) * 0.5, (-3.0 * cube + 4.0 * square + fraction) * 0.5, (cube - square) * 0.5)

def interp_matrix(lower, fraction, coarse_count):
    coarse = jnp.arange(coarse_count, dtype=jnp.int32)[:, None]
    weights = cubic_weights(fraction)
    matrix = jnp.zeros((coarse_count, lower.shape[0]), jnp.float32)
    for offset, weight in zip(range(-1, 3), weights):
        target = jnp.mod(lower + offset, coarse_count)
        matrix = matrix + jnp.where(coarse == target[None, :], weight[None, :], 0.0)
    return matrix

def rate(field, along_x, along_y):
    diffusivity = kappa_base * (1.0 + field * field)
    tendency = -0.5 * along_x * (jnp.roll(field, -1, 2) - jnp.roll(field, 1, 2))
    tendency = tendency - 0.5 * along_y * (jnp.roll(field, -1, 1) - jnp.roll(field, 1, 1))
    for direction in (0, 1, 2):
        face_flux = 0.5 * (diffusivity + jnp.roll(diffusivity, -1, direction)) * (jnp.roll(field, -1, direction) - field)
        tendency = tendency + face_flux - jnp.roll(face_flux, 1, direction)
    return tendency

def reference(velocity_modes, scalar, nest_shift):
    wave_x = signed_mode(jnp.arange(KX, dtype=jnp.int32), KX)
    wave_y = signed_mode(jnp.arange(KY, dtype=jnp.int32), KY)
    synth_x = hartley_table(wave_x[:, None], jnp.arange(NPX, dtype=jnp.int32)[None, :], NPX)
    synth_y = hartley_table(wave_y[:, None], jnp.arange(NPY, dtype=jnp.int32)[None, :], NPY)
    spaced = jnp.einsum('czkq,qy->czky', velocity_modes, synth_y, precision=highest)
    spaced = jnp.einsum('czky,kx->czyx', spaced, synth_x, precision=highest)
    along_x = spaced[0]
    along_y = spaced[1]
    products = jnp.stack([along_x * along_x - along_y * along_y, along_x * along_y])
    half_done = jnp.einsum('czyx,kx->czyk', products, synth_x / math.sqrt(NPX), precision=highest)
    stress = jnp.einsum('czyk,qy->czkq', half_done, synth_y / math.sqrt(NPY), precision=highest).astype(jnp.bfloat16)
    shift_cells = nest_shift[0]
    numer_x = 3 * (2 * jnp.arange(FX, dtype=jnp.int32) + 1 + 2 * shift_cells)
    matrix_x = interp_matrix(numer_x // 8, (numer_x % 8).astype(jnp.float32) / 8.0, NPX)
    numer_y = 3 * (2 * jnp.arange(FY, dtype=jnp.int32) + 1)
    matrix_y = interp_matrix(numer_y // 8, (numer_y % 8).astype(jnp.float32) / 8.0, NPY)
    numer_z = 2 * jnp.arange(FZ, dtype=jnp.int32) - 1
    matrix_z = interp_matrix(jnp.floor_divide(numer_z, 4), jnp.mod(numer_z, 4).astype(jnp.float32) / 4.0, CZ)
    fine_speed = jnp.einsum('czyx,xi->czyi', spaced, matrix_x, precision=highest)
    fine_speed = jnp.einsum('czyi,yj->czji', fine_speed, matrix_y, precision=highest)
    fine_speed = jnp.einsum('czji,zk->ckji', fine_speed, matrix_z, precision=highest)
    section = scalar + time_step * rate(scalar, fine_speed[0], fine_speed[1])
    scalar_next = 0.5 * (scalar + section + time_step * rate(section, fine_speed[0], fine_speed[1]))
    return (stress, scalar_next)
```

```python
import functools
import math

import jax
import jax.numpy as jnp
import numpy as np
from jax import lax
from jax.experimental import pallas as pl
from jax.experimental.pallas import tpu as pltpu
from jax.sharding import PartitionSpec as P

time_step = 0.2
edge = 4
margin = 16


def signed_modes(length):
    number = np.arange(length)
    return np.where(number < length // 2, number, number - length)


def hartley_table(modes, points, length):
    phase = np.mod(modes[:, None] * points[None, :], length) * (2.0 * math.pi / length)
    return (np.cos(phase) + np.sin(phase)).astype(np.float32)


def cubic_weights(fraction):
    square = fraction * fraction
    cube = square * fraction
    return (
        (-cube + 2.0 * square - fraction) * 0.5,
        (3.0 * cube - 5.0 * square + 2.0) * 0.5,
        (-3.0 * cube + 4.0 * square + fraction) * 0.5,
        (cube - square) * 0.5,
    )


def interp_matrix(lower, fraction, coarse_count):
    coarse = jnp.arange(coarse_count, dtype=jnp.int32)[:, None]
    matrix = jnp.zeros((coarse_count, lower.shape[0]), jnp.float32)
    for offset, weight in zip(range(-1, 3), cubic_weights(fraction)):
        target = jnp.mod(lower + offset, coarse_count)
        matrix = matrix + jnp.where(coarse == target[None, :], weight[None, :], 0.0)
    return matrix


def split(value):
    high = value.astype(jnp.bfloat16)
    return high, (value - high.astype(jnp.float32)).astype(jnp.bfloat16)


def dot3(left, right, contract):
    dims = (contract, ((), ()))
    product = functools.partial(
        lax.dot_general, dimension_numbers=dims, preferred_element_type=jnp.float32
    )
    return (
        product(left[0], right[1]) + product(left[1], right[0]) + product(left[0], right[0])
    )


rows_by_columns = ((1,), (0,))
rows_by_rows = ((1,), (1,))


def stress_kernel(planes, kx, block_ref, table_ref, out_ref, gathered):
    pencils = block_ref.shape[0]
    rows = out_ref.shape[1]
    table = split(table_ref[...])
    layers = planes // 2

    def spaced(plane):
        for s in range(pencils):
            gathered[:, s * kx : (s + 1) * kx] = block_ref[
                s, :rows, plane * kx : (plane + 1) * kx
            ]
        return dot3(split(gathered[...]), table, rows_by_columns)

    for layer in range(layers):
        u = spaced(layer)
        v = spaced(layers + layer)
        for c, product in ((0, u * u - v * v), (1, u * v)):
            half = dot3(split(product), table, rows_by_rows)
            plane = c * layers + layer
            for d in range(pencils):
                out_ref[d, :, plane * kx : (plane + 1) * kx] = half[:, d * kx : (d + 1) * kx]


def fine_kernel(layers, kx, own_ref, below_ref, above_ref, matrix_y_ref, synth_ref, out_ref, gathered, lines):
    pencils = own_ref.shape[0]
    synth = split(synth_ref[...])
    matrix_y = split(matrix_y_ref[...])
    for c in range(2):
        for p in range(layers + 4):
            if p < 2:
                ref, layer = below_ref, layers - 2 + p
            elif p < 2 + layers:
                ref, layer = own_ref, p - 2
            else:
                ref, layer = above_ref, p - 2 - layers
            plane = c * layers + layer
            for s in range(pencils):
                gathered[:, s * kx : (s + 1) * kx] = ref[s, :, plane * kx : (plane + 1) * kx]
            lines[p] = dot3(matrix_y, split(gathered[...]), rows_by_columns)
        for k in range(-1, 2 * layers + 1):
            lower = (2 * k - 1) // 4
            weights = cubic_weights(((2 * k - 1) % 4) / 4.0)
            mixed = weights[0] * lines[lower + 1]
            for offset in range(1, 4):
                mixed = mixed + weights[offset] * lines[lower + 1 + offset]
            out_ref[c, k + 1] = dot3(split(mixed), synth, rows_by_columns)


def heun_kernel(own_ref, before_ref, after_ref, below_ref, above_ref, speed_ref, out_ref, field, section):
    layers, rows, width = own_ref.shape
    end = margin + rows
    for z in range(layers):
        field[z + 2, margin:end] = own_ref[z]
        field[z + 2, margin - 2 : margin] = before_ref[z]
        field[z + 2, end : end + 2] = after_ref[z]
    for z in range(2):
        for at, ref in ((z, below_ref), (z + layers + 2, above_ref)):
            field[at, margin:end] = ref[z, :rows]
            field[at, end : end + 2] = ref[z, rows : rows + 2]
            field[at, margin - 2 : margin] = ref[z, rows + 2 : rows + 4]

    def rate(source, z, row, speed_z):
        middle = source[z, pl.ds(row, 8), :]
        previous = source[z, pl.ds(row - 8, 8), :]
        following = source[z, pl.ds(row + 8, 8), :]
        sublane = lax.broadcasted_iota(jnp.int32, (8, width), 0)
        north = pltpu.roll(jnp.where(sublane == 0, following, middle), 7, 0)
        south = pltpu.roll(jnp.where(sublane == 7, previous, middle), 1, 0)
        east = pltpu.roll(middle, width - 1, 1)
        west = pltpu.roll(middle, 1, 1)
        speed_row = row - (margin - 8)
        tendency = (-0.5 * speed_ref[0, speed_z, pl.ds(speed_row, 8), :]) * (east - west)
        tendency = tendency - (0.5 * speed_ref[1, speed_z, pl.ds(speed_row, 8), :]) * (north - south)
        base = 2.0 + middle * middle
        upper = source[z + 1, pl.ds(row, 8), :]
        lower = source[z - 1, pl.ds(row, 8), :]
        flux = None
        for other in (east, west, north, south, upper, lower):
            term = (base + other * other) * (other - middle)
            flux = term if flux is None else flux + term
        return middle, tendency + 0.05 * flux

    first_chunks = rows // 8 + 2

    def first(step, _):
        z = step // first_chunks + 1
        row = pl.multiple_of((step % first_chunks) * 8 + margin - 8, 8)
        middle, tendency = rate(field, z, row, z - 1)
        section[z - 1, pl.ds(row, 8), :] = middle + time_step * tendency
        return 0

    lax.fori_loop(0, (layers + 2) * first_chunks, first, 0)
    chunks = rows // 8

    def second(step, _):
        z = step // chunks
        row = pl.multiple_of((step % chunks) * 8 + margin, 8)
        middle, tendency = rate(section, z + 1, row, z + 1)
        own = own_ref[z, pl.ds(row - margin, 8), :]
        out_ref[z, pl.ds(row - margin, 8), :] = 0.5 * (own + middle + time_step * tendency)
        return 0

    lax.fori_loop(0, layers * chunks, second, 0)


def in_vmem(kernel, shape, count, scratch, flops):
    spec = pl.BlockSpec(memory_space=pltpu.VMEM)
    return pl.pallas_call(
        kernel,
        out_shape=jax.ShapeDtypeStruct(shape, jnp.float32),
        in_specs=[spec] * count,
        out_specs=spec,
        scratch_shapes=scratch,
        compiler_params=pltpu.CompilerParams(vmem_limit_bytes=56 * 1024 * 1024),
        cost_estimate=pl.CostEstimate(flops=flops, bytes_accessed=4 * 1024 * 1024, transcendentals=0),
    )


def shards(velocity_modes, scalar, nest_shift):
    pencils = lax.axis_size("wa")
    slabs = lax.axis_size("gz")
    _, layers, kx, ky_count = velocity_modes.shape
    kx_count = kx * pencils
    fine_layers, fine_rows, fine_x = scalar.shape
    padded_x = 3 * kx_count // 2
    padded_y = 3 * ky_count // 2
    y_local = padded_y // pencils
    rows = y_local + 2 * edge
    planes = 2 * layers

    order = np.concatenate([np.arange(y_local + edge), np.arange(-edge, 0)])
    y_points = (y_local * np.arange(pencils)[:, None] + order[None, :]).reshape(-1) % padded_y
    synth_y = jnp.asarray(hartley_table(signed_modes(ky_count), y_points, padded_y)).reshape(
        ky_count, pencils, rows
    )
    analysis_y = jnp.asarray(
        hartley_table(signed_modes(ky_count), np.arange(padded_y), padded_y)
    ).reshape(ky_count, pencils, y_local)
    synth_x = jnp.asarray(hartley_table(signed_modes(kx_count), np.arange(padded_x), padded_x))

    speed_rows = fine_rows + 16
    matrix_y = np.zeros((speed_rows, rows), np.float32)
    place = {int(r): i for i, r in enumerate(order)}
    for j in range(-1, fine_rows + 1):
        numer = 3 * (2 * j + 1)
        for offset, weight in zip(range(-1, 3), cubic_weights((numer % 8) / 8.0)):
            matrix_y[j + 8, place[numer // 8 + offset]] += weight

    def ring(axis, count, value, step):
        return lax.ppermute(value, axis, [(i, (i + step) % count) for i in range(count)])

    modes_below = ring("gz", slabs, velocity_modes, 1)
    modes_above = ring("gz", slabs, velocity_modes, -1)
    before = ring("wa", pencils, scalar[:, -2:], 1)
    after = ring("wa", pencils, scalar[:, :2], -1)

    def to_rows(modes):
        lines = jnp.einsum(
            "nq,qdr->drn", modes.reshape(planes * kx, ky_count), synth_y, precision=lax.Precision.HIGH
        )
        return lax.all_to_all(lines, "wa", split_axis=0, concat_axis=0, tiled=True)

    own = to_rows(velocity_modes)
    half_done = in_vmem(
        functools.partial(stress_kernel, planes, kx),
        (pencils, y_local, planes * kx),
        2,
        [pltpu.VMEM((y_local, kx_count), jnp.float32)],
        12 * planes * y_local * kx_count * padded_x,
    )(own, synth_x)
    returned = lax.all_to_all(half_done, "wa", split_axis=0, concat_axis=0, tiled=True)
    stress = jnp.einsum("syn,qsy->nq", returned, analysis_y, precision=lax.Precision.HIGH)
    stress = (stress * (1.0 / math.sqrt(padded_x * padded_y))).astype(jnp.bfloat16)
    stress = stress.reshape(2, layers, kx, ky_count)

    numer_x = 3 * (2 * jnp.arange(fine_x, dtype=jnp.int32) + 1 + 2 * nest_shift[0])
    matrix_x = interp_matrix(numer_x // 8, (numer_x % 8).astype(jnp.float32) / 8.0, padded_x)
    synth_fine = jnp.dot(synth_x, matrix_x, precision=lax.Precision.HIGH)

    top = jnp.concatenate([scalar[-2:], after[-2:], before[-2:]], axis=1)
    bottom = jnp.concatenate([scalar[:2], after[:2], before[:2]], axis=1)
    below = ring("gz", slabs, top, 1)
    above = ring("gz", slabs, bottom, -1)

    speed = in_vmem(
        functools.partial(fine_kernel, layers, kx),
        (2, fine_layers + 2, speed_rows, fine_x),
        5,
        [
            pltpu.VMEM((rows, kx_count), jnp.float32),
            pltpu.VMEM((layers + 4, speed_rows, kx_count), jnp.float32),
        ],
        12 * (fine_layers + 2) * speed_rows * kx_count * fine_x,
    )(own, to_rows(modes_below), to_rows(modes_above), jnp.asarray(matrix_y), synth_fine)

    scalar_next = in_vmem(
        heun_kernel,
        scalar.shape,
        6,
        [
            pltpu.VMEM((fine_layers + 4, fine_rows + 2 * margin, fine_x), jnp.float32),
            pltpu.VMEM((fine_layers + 2, fine_rows + 2 * margin, fine_x), jnp.float32),
        ],
        100 * fine_layers * fine_rows * fine_x,
    )(scalar, before, after, below, above, speed)
    return (stress, scalar_next)


def solution(mesh):
    placed = (P(None, "gz", "wa", None), P("gz", "wa", None), P())
    return jax.shard_map(
        shards,
        mesh=mesh,
        in_specs=placed,
        out_specs=(P(None, "gz", "wa", None), P("gz", "wa", None)),
        check_vma=False,
    )
```

```python
import functools
import math

import jax
import jax.numpy as jnp
import numpy as np
from jax import lax
from jax.experimental import pallas as pl
from jax.experimental.pallas import tpu as pltpu
from jax.sharding import PartitionSpec as P


time_step = 0.2
edge = 4
margin = 16


def signed_modes(length):
    number = np.arange(length)
    return np.where(number < length // 2, number, number - length)


def hartley_table(modes, points, length):
    phase = np.mod(modes[:, None] * points[None, :], length) * (2.0 * math.pi / length)
    return (np.cos(phase) + np.sin(phase)).astype(np.float32)


def cubic_weights(fraction):
    square = fraction * fraction
    cube = square * fraction
    return (
        (-cube + 2.0 * square - fraction) * 0.5,
        (3.0 * cube - 5.0 * square + 2.0) * 0.5,
        (-3.0 * cube + 4.0 * square + fraction) * 0.5,
        (cube - square) * 0.5,
    )


def interp_matrix(lower, fraction, coarse_count):
    coarse = jnp.arange(coarse_count, dtype=jnp.int32)[:, None]
    matrix = jnp.zeros((coarse_count, lower.shape[0]), jnp.float32)
    for offset, weight in zip(range(-1, 3), cubic_weights(fraction)):
        target = jnp.mod(lower + offset, coarse_count)
        matrix = matrix + jnp.where(coarse == target[None, :], weight[None, :], 0.0)
    return matrix


def split(value):
    high = value.astype(jnp.bfloat16)
    return high, (value - high.astype(jnp.float32)).astype(jnp.bfloat16)


def dot3(left, right, contract):
    dims = (contract, ((), ()))
    product = functools.partial(
        lax.dot_general, dimension_numbers=dims, preferred_element_type=jnp.float32
    )
    return (
        product(left[0], right[1]) + product(left[1], right[0]) + product(left[0], right[0])
    )


rows_by_columns = ((1,), (0,))
rows_by_rows = ((1,), (1,))


def stress_kernel(planes, kx, block_ref, table_ref, out_ref, gathered):
    pencils = block_ref.shape[0]
    rows = out_ref.shape[1]
    table = split(table_ref[...])
    layers = planes // 2

    def spaced(plane):
        for s in range(pencils):
            gathered[:, s * kx : (s + 1) * kx] = block_ref[
                s, :rows, plane * kx : (plane + 1) * kx
            ]
        return dot3(split(gathered[...]), table, rows_by_columns)

    for layer in range(layers):
        u = spaced(layer)
        v = spaced(layers + layer)
        for c, product in ((0, u * u - v * v), (1, u * v)):
            half = dot3(split(product), table, rows_by_rows)
            plane = c * layers + layer
            for d in range(pencils):
                out_ref[d, :, plane * kx : (plane + 1) * kx] = half[:, d * kx : (d + 1) * kx]


def fine_kernel(layers, kx, own_ref, halo_ref, matrix_y_ref, synth_ref, out_ref, gathered, lines):
    pencils = own_ref.shape[0]
    synth = split(synth_ref[...])
    matrix_y = split(matrix_y_ref[...])
    for c in range(2):
        for p in range(layers + 4):
            if p < 2:
                ref, plane = halo_ref, c * layers + layers - 2 + p
            elif p < 2 + layers:
                ref, plane = own_ref, c * layers + p - 2
            else:
                ref, plane = halo_ref, (2 + c) * layers + p - 2 - layers
            for s in range(pencils):
                gathered[:, s * kx : (s + 1) * kx] = ref[s, :, plane * kx : (plane + 1) * kx]
            lines[p] = dot3(matrix_y, split(gathered[...]), rows_by_columns)
        for k in range(-1, 2 * layers + 1):
            lower = (2 * k - 1) // 4
            weights = [-0.5 * time_step * w for w in cubic_weights(((2 * k - 1) % 4) / 4.0)]
            mixed = weights[0] * lines[lower + 1]
            for offset in range(1, 4):
                mixed = mixed + weights[offset] * lines[lower + 1 + offset]
            out_ref[c, k + 1] = dot3(split(mixed), synth, rows_by_columns)


def pack_kernel(scalar_ref, before_ref, after_ref, top_ref, bottom_ref):
    layers, rows, _ = scalar_ref.shape
    for z in range(2):
        for source, ref in ((layers - 2 + z, top_ref), (z, bottom_ref)):
            ref[z * rows : (z + 1) * rows] = scalar_ref[source]
            side = 2 * rows + 4 * z
            ref[side : side + 2] = after_ref[source]
            ref[side + 2 : side + 4] = before_ref[source]


def heun_kernel(own_ref, before_ref, after_ref, below_ref, above_ref, speed_ref, out_ref, field, section):
    layers, rows, width = own_ref.shape
    end = margin + rows
    for z in range(layers):
        field[z + 2, margin:end] = own_ref[z]
        field[z + 2, margin - 2 : margin] = before_ref[z]
        field[z + 2, end : end + 2] = after_ref[z]
    for z in range(2):
        for at, ref in ((z, below_ref), (z + layers + 2, above_ref)):
            side = 2 * rows + 4 * z
            field[at, margin:end] = ref[z * rows : (z + 1) * rows]
            field[at, end : end + 2] = ref[side : side + 2]
            field[at, margin - 2 : margin] = ref[side + 2 : side + 4]
    sublane = lax.broadcasted_iota(jnp.int32, (8, width), 0)

    def sweep(source, depth, row, speed_at, store):
        speed_row = pl.multiple_of(row - (margin - 8), 8)
        lower = source[0, pl.ds(row, 8), :]
        middle = source[1, pl.ds(row, 8), :]
        base = 2.0 + middle * middle
        difference = middle - lower
        below = (base + lower * lower) * difference
        for z in range(1, depth - 1):
            upper = source[z + 1, pl.ds(row, 8), :]
            square = upper * upper
            above = (base + square) * (upper - middle)
            flux = above - below
            previous = source[z, pl.ds(row - 8, 8), :]
            following = source[z, pl.ds(row + 8, 8), :]
            north = pltpu.roll(jnp.where(sublane == 0, following, middle), 7, 0)
            south = pltpu.roll(jnp.where(sublane == 7, previous, middle), 1, 0)
            flux = flux + (base + north * north) * (north - middle)
            flux = flux + (base + south * south) * (south - middle)
            tendency = speed_ref[1, z + speed_at, pl.ds(speed_row, 8), :] * (north - south)
            east = pltpu.roll(middle, width - 1, 1)
            west = pltpu.roll(middle, 1, 1)
            face = (base + east * east) * (east - middle)
            flux = flux + (face - pltpu.roll(face, 1, 1))
            tendency = tendency + speed_ref[0, z + speed_at, pl.ds(speed_row, 8), :] * (east - west)
            store(z, middle, tendency + (0.05 * time_step) * flux)
            middle, base, below = upper, 2.0 + square, above

    def first(step, _):
        row = pl.multiple_of(step * 8 + margin - 8, 8)

        def store(z, middle, change):
            section[z - 1, pl.ds(row, 8), :] = middle + change

        sweep(field, layers + 4, row, -1, store)
        return 0

    lax.fori_loop(0, rows // 8 + 2, first, 0)

    def second(step, _):
        row = pl.multiple_of(step * 8 + margin, 8)
        out_row = pl.multiple_of(step * 8, 8)

        def store(z, middle, change):
            own = own_ref[z - 1, pl.ds(out_row, 8), :]
            out_ref[z - 1, pl.ds(out_row, 8), :] = 0.5 * (own + middle + change)

        sweep(section, layers + 2, row, 0, store)
        return 0

    lax.fori_loop(0, rows // 8, second, 0)


def in_vmem(kernel, shapes, count, scratch, flops, mebibytes):
    spec = pl.BlockSpec(memory_space=pltpu.VMEM)
    return pl.pallas_call(
        kernel,
        out_shape=[jax.ShapeDtypeStruct(shape, jnp.float32) for shape in shapes],
        in_specs=[spec] * count,
        out_specs=[spec] * len(shapes),
        scratch_shapes=scratch,
        compiler_params=pltpu.CompilerParams(vmem_limit_bytes=mebibytes * 1024 * 1024),
        cost_estimate=pl.CostEstimate(flops=flops, bytes_accessed=4 * 1024 * 1024, transcendentals=0),
    )


def shards(velocity_modes, scalar, nest_shift):
    pencils = lax.axis_size("wa")
    slabs = lax.axis_size("gz")
    _, layers, kx, ky_count = velocity_modes.shape
    kx_count = kx * pencils
    fine_layers, fine_rows, fine_x = scalar.shape
    padded_x = 3 * kx_count // 2
    padded_y = 3 * ky_count // 2
    y_local = padded_y // pencils
    rows = y_local + 2 * edge
    planes = 2 * layers

    order = np.concatenate([np.arange(y_local + edge), np.arange(-edge, 0)])
    y_points = (y_local * np.arange(pencils)[:, None] + order[None, :]).reshape(-1) % padded_y
    synth_y = jnp.asarray(hartley_table(signed_modes(ky_count), y_points, padded_y)).reshape(
        ky_count, pencils, rows
    )
    analysis_y = jnp.asarray(
        hartley_table(signed_modes(ky_count), np.arange(padded_y), padded_y)
    ).reshape(ky_count, pencils, y_local)
    synth_x = jnp.asarray(hartley_table(signed_modes(kx_count), np.arange(padded_x), padded_x))

    speed_rows = fine_rows + 16
    matrix_y = np.zeros((speed_rows, rows), np.float32)
    place = {int(r): i for i, r in enumerate(order)}
    for j in range(-1, fine_rows + 1):
        numer = 3 * (2 * j + 1)
        for offset, weight in zip(range(-1, 3), cubic_weights((numer % 8) / 8.0)):
            matrix_y[j + 8, place[numer // 8 + offset]] += weight

    def ring(axis, count, value, step):
        return lax.ppermute(value, axis, [(i, (i + step) % count) for i in range(count)])

    modes_below = ring("gz", slabs, velocity_modes, 1)
    modes_above = ring("gz", slabs, velocity_modes, -1)
    before = ring("wa", pencils, scalar[:, -2:], 1)
    after = ring("wa", pencils, scalar[:, :2], -1)
    packed = (2 * fine_rows + 8, fine_x)
    top, bottom = in_vmem(pack_kernel, (packed, packed), 3, [], 10, 16)(scalar, before, after)
    below = ring("gz", slabs, top, 1)
    above = ring("gz", slabs, bottom, -1)

    def to_rows(modes):
        lines = jnp.einsum("nq,qdr->drn", modes, synth_y, precision=lax.Precision.HIGH)
        return lax.all_to_all(lines, "wa", split_axis=0, concat_axis=0, tiled=True)

    own = to_rows(velocity_modes.reshape(planes * kx, ky_count))
    (half_done,) = in_vmem(
        functools.partial(stress_kernel, planes, kx),
        ((pencils, y_local, planes * kx),),
        2,
        [pltpu.VMEM((y_local, kx_count), jnp.float32)],
        12 * planes * y_local * kx_count * padded_x,
        32,
    )(own, synth_x)
    returned = lax.all_to_all(half_done, "wa", split_axis=0, concat_axis=0, tiled=True)
    stress = jnp.einsum("syn,qsy->nq", returned, analysis_y, precision=lax.Precision.HIGH)
    stress = (stress * (1.0 / math.sqrt(padded_x * padded_y))).astype(jnp.bfloat16)
    stress = stress.reshape(2, layers, kx, ky_count)

    numer_x = 3 * (2 * jnp.arange(fine_x, dtype=jnp.int32) + 1 + 2 * nest_shift[0])
    matrix_x = interp_matrix(numer_x // 8, (numer_x % 8).astype(jnp.float32) / 8.0, padded_x)
    synth_fine = jnp.dot(synth_x, matrix_x, precision=lax.Precision.HIGH)

    halo = to_rows(
        jnp.concatenate([modes_below, modes_above]).reshape(2 * planes * kx, ky_count)
    )
    (speed,) = in_vmem(
        functools.partial(fine_kernel, layers, kx),
        ((2, fine_layers + 2, speed_rows, fine_x),),
        4,
        [
            pltpu.VMEM((rows, kx_count), jnp.float32),
            pltpu.VMEM((layers + 4, speed_rows, kx_count), jnp.float32),
        ],
        12 * (fine_layers + 2) * speed_rows * kx_count * fine_x,
        32,
    )(own, halo, jnp.asarray(matrix_y), synth_fine)

    (scalar_next,) = in_vmem(
        heun_kernel,
        (scalar.shape,),
        6,
        [
            pltpu.VMEM((fine_layers + 4, fine_rows + 2 * margin, fine_x), jnp.float32),
            pltpu.VMEM((fine_layers + 2, fine_rows + 2 * margin, fine_x), jnp.float32),
        ],
        100 * fine_layers * fine_rows * fine_x,
        32,
    )(scalar, before, after, below, above, speed)
    return (stress, scalar_next)


def solution(mesh):
    placed = (P(None, "gz", "wa", None), P("gz", "wa", None), P())
    return jax.shard_map(
        shards,
        mesh=mesh,
        in_specs=placed,
        out_specs=(P(None, "gz", "wa", None), P("gz", "wa", None)),
        check_vma=False,
    )
```

```python
import functools
import math

import jax
import jax.numpy as jnp
import numpy as np
from jax import lax
from jax.experimental import pallas as pl
from jax.experimental.pallas import tpu as pltpu
from jax.sharding import PartitionSpec as P


time_step = 0.2
edge = 4
margin = 16


def signed_modes(length):
    number = np.arange(length)
    return np.where(number < length // 2, number, number - length)


def hartley_table(modes, points, length):
    phase = np.mod(modes[:, None] * points[None, :], length) * (2.0 * math.pi / length)
    return (np.cos(phase) + np.sin(phase)).astype(np.float32)


def cubic_weights(fraction):
    square = fraction * fraction
    cube = square * fraction
    return (
        (-cube + 2.0 * square - fraction) * 0.5,
        (3.0 * cube - 5.0 * square + 2.0) * 0.5,
        (-3.0 * cube + 4.0 * square + fraction) * 0.5,
        (cube - square) * 0.5,
    )


def interp_matrix(lower, fraction, coarse_count):
    coarse = jnp.arange(coarse_count, dtype=jnp.int32)[:, None]
    matrix = jnp.zeros((coarse_count, lower.shape[0]), jnp.float32)
    for offset, weight in zip(range(-1, 3), cubic_weights(fraction)):
        target = jnp.mod(lower + offset, coarse_count)
        matrix = matrix + jnp.where(coarse == target[None, :], weight[None, :], 0.0)
    return matrix


def split(value):
    high = value.astype(jnp.bfloat16)
    return high, (value - high.astype(jnp.float32)).astype(jnp.bfloat16)


def dot3(left, right, contract):
    dims = (contract, ((), ()))
    product = functools.partial(
        lax.dot_general, dimension_numbers=dims, preferred_element_type=jnp.float32
    )
    return (
        product(left[0], right[1]) + product(left[1], right[0]) + product(left[0], right[0])
    )


rows_by_columns = ((1,), (0,))
rows_by_rows = ((1,), (1,))


def stress_kernel(planes, kx, block_ref, table_ref, out_ref, gathered):
    pencils = block_ref.shape[0]
    rows = out_ref.shape[1]
    table = split(table_ref[...])
    layers = planes // 2

    def spaced(plane):
        for s in range(pencils):
            gathered[:, s * kx : (s + 1) * kx] = block_ref[
                s, :rows, plane * kx : (plane + 1) * kx
            ]
        return dot3(split(gathered[...]), table, rows_by_columns)

    for layer in range(layers):
        u = spaced(layer)
        v = spaced(layers + layer)
        for c, product in ((0, u * u - v * v), (1, u * v)):
            half = dot3(split(product), table, rows_by_rows)
            plane = c * layers + layer
            for d in range(pencils):
                out_ref[d, :, plane * kx : (plane + 1) * kx] = half[:, d * kx : (d + 1) * kx]


def fine_kernel(layers, kx, own_ref, halo_ref, matrix_y_ref, synth_ref, out_ref, gathered, lines):
    pencils = own_ref.shape[0]
    synth = split(synth_ref[...])
    matrix_y = split(matrix_y_ref[...])
    for c in range(2):
        for p in range(layers + 4):
            if p < 2:
                ref, plane = halo_ref, c * layers + layers - 2 + p
            elif p < 2 + layers:
                ref, plane = own_ref, c * layers + p - 2
            else:
                ref, plane = halo_ref, (2 + c) * layers + p - 2 - layers
            for s in range(pencils):
                gathered[:, s * kx : (s + 1) * kx] = ref[s, :, plane * kx : (plane + 1) * kx]
            lines[p] = dot3(matrix_y, split(gathered[...]), rows_by_columns)
        for k in range(-1, 2 * layers + 1):
            lower = (2 * k - 1) // 4
            weights = [-0.5 * time_step * w for w in cubic_weights(((2 * k - 1) % 4) / 4.0)]
            mixed = weights[0] * lines[lower + 1]
            for offset in range(1, 4):
                mixed = mixed + weights[offset] * lines[lower + 1 + offset]
            out_ref[c, k + 1] = dot3(split(mixed), synth, rows_by_columns)


def pack_kernel(scalar_ref, before_ref, after_ref, top_ref, bottom_ref):
    layers, rows, _ = scalar_ref.shape
    for z in range(2):
        for source, ref in ((layers - 2 + z, top_ref), (z, bottom_ref)):
            ref[z * rows : (z + 1) * rows] = scalar_ref[source]
            side = 2 * rows + 4 * z
            ref[side : side + 2] = after_ref[source]
            ref[side + 2 : side + 4] = before_ref[source]


def heun_kernel(own_ref, before_ref, after_ref, below_ref, above_ref, speed_ref, out_ref, field, section):
    layers, rows, width = own_ref.shape
    end = margin + rows
    for z in range(layers):
        field[z + 2, margin:end] = own_ref[z]
        field[z + 2, margin - 2 : margin] = before_ref[z]
        field[z + 2, end : end + 2] = after_ref[z]
    for z in range(2):
        for at, ref in ((z, below_ref), (z + layers + 2, above_ref)):
            side = 2 * rows + 4 * z
            field[at, margin:end] = ref[z * rows : (z + 1) * rows]
            field[at, end : end + 2] = ref[side : side + 2]
            field[at, margin - 2 : margin] = ref[side + 2 : side + 4]
    sublane = lax.broadcasted_iota(jnp.int32, (8, width), 0)

    def sweep(source, depth, row, speed_at, store):
        speed_row = pl.multiple_of(row - (margin - 8), 8)
        lower = source[0, pl.ds(row, 8), :]
        middle = source[1, pl.ds(row, 8), :]
        base = 2.0 + middle * middle
        difference = middle - lower
        below = (base + lower * lower) * difference
        for z in range(1, depth - 1):
            upper = source[z + 1, pl.ds(row, 8), :]
            square = upper * upper
            above = (base + square) * (upper - middle)
            flux = above - below
            previous = source[z, pl.ds(row - 8, 8), :]
            following = source[z, pl.ds(row + 8, 8), :]
            north = pltpu.roll(jnp.where(sublane == 0, following, middle), 7, 0)
            south = pltpu.roll(jnp.where(sublane == 7, previous, middle), 1, 0)
            flux = flux + (base + north * north) * (north - middle)
            flux = flux + (base + south * south) * (south - middle)
            tendency = speed_ref[1, z + speed_at, pl.ds(speed_row, 8), :] * (north - south)
            east = pltpu.roll(middle, width - 1, 1)
            west = pltpu.roll(middle, 1, 1)
            face = (base + east * east) * (east - middle)
            flux = flux + (face - pltpu.roll(face, 1, 1))
            tendency = tendency + speed_ref[0, z + speed_at, pl.ds(speed_row, 8), :] * (east - west)
            store(z, middle, tendency + (0.05 * time_step) * flux)
            middle, base, below = upper, 2.0 + square, above

    def first(step, _):
        row = pl.multiple_of(step * 8 + margin - 8, 8)

        def store(z, middle, change):
            section[z - 1, pl.ds(row, 8), :] = middle + change

        sweep(field, layers + 4, row, -1, store)
        return 0

    lax.fori_loop(0, rows // 8 + 2, first, 0, unroll=2)

    def second(step, _):
        row = pl.multiple_of(step * 8 + margin, 8)
        out_row = pl.multiple_of(step * 8, 8)

        def store(z, middle, change):
            own = own_ref[z - 1, pl.ds(out_row, 8), :]
            out_ref[z - 1, pl.ds(out_row, 8), :] = 0.5 * (own + middle + change)

        sweep(section, layers + 2, row, 0, store)
        return 0

    lax.fori_loop(0, rows // 8, second, 0, unroll=2)


def in_vmem(kernel, shapes, count, scratch, flops, mebibytes):
    spec = pl.BlockSpec(memory_space=pltpu.VMEM)
    return pl.pallas_call(
        kernel,
        out_shape=[jax.ShapeDtypeStruct(shape, jnp.float32) for shape in shapes],
        in_specs=[spec] * count,
        out_specs=[spec] * len(shapes),
        scratch_shapes=scratch,
        compiler_params=pltpu.CompilerParams(vmem_limit_bytes=mebibytes * 1024 * 1024),
        cost_estimate=pl.CostEstimate(flops=flops, bytes_accessed=4 * 1024 * 1024, transcendentals=0),
    )


def shards(velocity_modes, scalar, nest_shift):
    pencils = lax.axis_size("wa")
    slabs = lax.axis_size("gz")
    _, layers, kx, ky_count = velocity_modes.shape
    kx_count = kx * pencils
    fine_layers, fine_rows, fine_x = scalar.shape
    padded_x = 3 * kx_count // 2
    padded_y = 3 * ky_count // 2
    y_local = padded_y // pencils
    rows = y_local + 2 * edge
    planes = 2 * layers

    order = np.concatenate([np.arange(y_local + edge), np.arange(-edge, 0)])
    y_points = (y_local * np.arange(pencils)[:, None] + order[None, :]).reshape(-1) % padded_y
    synth_y = jnp.asarray(hartley_table(signed_modes(ky_count), y_points, padded_y)).reshape(
        ky_count, pencils, rows
    )
    analysis_y = jnp.asarray(
        hartley_table(signed_modes(ky_count), np.arange(padded_y), padded_y)
    ).reshape(ky_count, pencils, y_local)
    synth_x = jnp.asarray(hartley_table(signed_modes(kx_count), np.arange(padded_x), padded_x))

    speed_rows = fine_rows + 16
    matrix_y = np.zeros((speed_rows, rows), np.float32)
    place = {int(r): i for i, r in enumerate(order)}
    for j in range(-1, fine_rows + 1):
        numer = 3 * (2 * j + 1)
        for offset, weight in zip(range(-1, 3), cubic_weights((numer % 8) / 8.0)):
            matrix_y[j + 8, place[numer // 8 + offset]] += weight

    def ring(axis, count, value, step):
        return lax.ppermute(value, axis, [(i, (i + step) % count) for i in range(count)])

    modes_below = ring("gz", slabs, velocity_modes, 1)
    modes_above = ring("gz", slabs, velocity_modes, -1)
    before = ring("wa", pencils, scalar[:, -2:], 1)
    after = ring("wa", pencils, scalar[:, :2], -1)
    packed = (2 * fine_rows + 8, fine_x)
    top, bottom = in_vmem(pack_kernel, (packed, packed), 3, [], 10, 16)(scalar, before, after)
    below = ring("gz", slabs, top, 1)
    above = ring("gz", slabs, bottom, -1)

    def to_rows(modes):
        lines = jnp.einsum("nq,qdr->drn", modes, synth_y, precision=lax.Precision.HIGH)
        return lax.all_to_all(lines, "wa", split_axis=0, concat_axis=0, tiled=True)

    own = to_rows(velocity_modes.reshape(planes * kx, ky_count))
    (half_done,) = in_vmem(
        functools.partial(stress_kernel, planes, kx),
        ((pencils, y_local, planes * kx),),
        2,
        [pltpu.VMEM((y_local, kx_count), jnp.float32)],
        12 * planes * y_local * kx_count * padded_x,
        32,
    )(own, synth_x)
    returned = lax.all_to_all(half_done, "wa", split_axis=0, concat_axis=0, tiled=True)
    stress = jnp.einsum("syn,qsy->nq", returned, analysis_y, precision=lax.Precision.HIGH)
    stress = (stress * (1.0 / math.sqrt(padded_x * padded_y))).astype(jnp.bfloat16)
    stress = stress.reshape(2, layers, kx, ky_count)

    numer_x = 3 * (2 * jnp.arange(fine_x, dtype=jnp.int32) + 1 + 2 * nest_shift[0])
    matrix_x = interp_matrix(numer_x // 8, (numer_x % 8).astype(jnp.float32) / 8.0, padded_x)
    synth_fine = jnp.dot(synth_x, matrix_x, precision=lax.Precision.HIGH)

    halo = to_rows(jnp.concatenate([modes_below, modes_above]).reshape(2 * planes * kx, ky_count))
    (speed,) = in_vmem(
        functools.partial(fine_kernel, layers, kx),
        ((2, fine_layers + 2, speed_rows, fine_x),),
        4,
        [
            pltpu.VMEM((rows, kx_count), jnp.float32),
            pltpu.VMEM((layers + 4, speed_rows, kx_count), jnp.float32),
        ],
        12 * (fine_layers + 2) * speed_rows * kx_count * fine_x,
        32,
    )(own, halo, jnp.asarray(matrix_y), synth_fine)

    (scalar_next,) = in_vmem(
        heun_kernel,
        (scalar.shape,),
        6,
        [
            pltpu.VMEM((fine_layers + 4, fine_rows + 2 * margin, fine_x), jnp.float32),
            pltpu.VMEM((fine_layers + 2, fine_rows + 2 * margin, fine_x), jnp.float32),
        ],
        100 * fine_layers * fine_rows * fine_x,
        32,
    )(scalar, before, after, below, above, speed)
    return (stress, scalar_next)


def solution(mesh):
    placed = (P(None, "gz", "wa", None), P("gz", "wa", None), P())
    return jax.shard_map(
        shards,
        mesh=mesh,
        in_specs=placed,
        out_specs=(P(None, "gz", "wa", None), P("gz", "wa", None)),
        check_vma=False,
    )
```
